32 devices in a mesh: lat: 16 (over z, x, core), wid: 2 (over y).
Axes of the slice: x: 2, y: 2, z: 4, core: 2. Of those that a mesh axis runs over, the one named last changes fastest.
Arguments:
- buffer_src: bfloat16 [1728, 3584], P('lat', 'wid'), may hold values from -6 to 6
- buffer_tgt: bfloat16 [1728, 3, 3584], P('lat', None, 'wid'), may hold values from -6 to 6
- batch_rows: int32 [1536], replicated, may hold values from 0 to 1727, as said below
- enc_w: float32 [3584, 8192], P('wid', 'lat'), may hold values from -0.09375 to 0.09375
- enc_b: float32 [8192], P('lat'), may hold values from -3 to 3
- dec_w: float32 [3, 8192, 3584], P(None, 'lat', 'wid'), may hold values from -0.0625 to 0.0625
- dec_b: float32 [3, 3584], P(None, 'wid'), may hold values from -3 to 3
- enc_m: float32 [3584, 8192], P('wid', 'lat'), may hold values from -40 to 40
- enc_v: float32 [3584, 8192], P('wid', 'lat'), may hold values from 3 to 300
- dec_m: float32 [3, 8192, 3584], P(None, 'lat', 'wid'), may hold values from -20 to 20
- dec_v: float32 [3, 8192, 3584], P(None, 'lat', 'wid'), may hold values from 3 to 300
Outputs:
- enc_w_new: float32 [3584, 8192], P('wid', 'lat')
- enc_m_new: float32 [3584, 8192], P('wid', 'lat')
- enc_v_new: float32 [3584, 8192], P('wid', 'lat')
- dec_w_new: float32 [3, 8192, 3584], P(None, 'lat', 'wid')
- dec_m_new: float32 [3, 8192, 3584], P(None, 'lat', 'wid')
- dec_v_new: float32 [3, 8192, 3584], P(None, 'lat', 'wid')
The draws below stay inside these ranges and needn't reach their ends.
Inputs may be any that keep to these rules, and one draw needn't show every extreme that they name: `batch_rows`: 1536 different rows of the buffer.
All inputs are finite; a program needn't handle non-finite values.
Results may differ from the reference program's by a relative error of at most 0.0035.
Values may be sent and summed in bfloat16 or wider, within the bound.
A program may use at most 256 MiB of HBM per device.

```python
import math
import jax
import jax.numpy as jnp

D = 3584
LATENTS = 8192
TARGETS = 3
STEP = 100
TOK = 1536
BUFFER = 1728


def draw_batch_rows(key, part):
    return jax.random.permutation(key, BUFFER)[:TOK].astype(jnp.int32)


def level_of(rng, extent, split, low, high):
    loudness = 1.0
    for dim, blocks in split:
        steps = jax.random.uniform(jax.random.fold_in(jax.random.fold_in(rng, 6), dim), (blocks,), jnp.float32, low / len(split), high / len(split))
        loudness = loudness * jnp.repeat(jnp.exp(steps), extent[dim] // blocks).reshape((-1,) + (1,) * (len(extent) - 1 - dim))
    return loudness


def centred(stream_key, shape, width, reach, split=(), kind=jnp.bfloat16):
    gain = level_of(stream_key, shape, split, -0.22, 0.18) if split else 1.0
    entries = jax.random.normal(stream_key, shape, jnp.float32) * width * gain
    return jnp.minimum(jnp.maximum(entries, -reach), reach).astype(kind)


def setup_inputs(seed: int = 0) -> dict:
    keys = jax.random.split(jax.random.key(seed), 12)
    return {
        "buffer_src": centred(keys[0], (BUFFER, D), 1.0, 6.0, ((0, 16), (1, 2))),
        "buffer_tgt": centred(keys[1], (BUFFER, TARGETS, D), 1.0, 6.0, ((0, 16), (2, 2))),
        "batch_rows": draw_batch_rows(jax.random.fold_in(keys[11], 71), 0),
        "enc_w": centred(keys[3], (D, LATENTS), D ** -0.5, 0.09375, ((0, 2), (1, 16)), jnp.float32),
        "enc_b": centred(keys[4], (LATENTS,), 0.5, 3.0, ((0, 16),), jnp.float32),
        "dec_w": centred(keys[5], (TARGETS, LATENTS, D), LATENTS ** -0.5, 0.0625, ((1, 16), (2, 2)), jnp.float32),
        "dec_b": centred(keys[6], (TARGETS, D), 0.5, 3.0, ((1, 2),), jnp.float32),
        "enc_m": centred(keys[7], (D, LATENTS), 10.0, 40.0, ((0, 2), (1, 16)), jnp.float32),
        "enc_v": jnp.clip(jnp.exp(math.log(300.0) - 4.6051702 * jax.random.uniform(keys[8], (D, LATENTS), jnp.float32) ** level_of(keys[8], (D, LATENTS), ((0, 2), (1, 16)), -0.2, 0.2)), 3.0, 300.0),
        "dec_m": centred(keys[9], (TARGETS, LATENTS, D), 5.0, 20.0, ((1, 16), (2, 2)), jnp.float32),
        "dec_v": jnp.clip(jnp.exp(math.log(300.0) - 4.6051702 * jax.random.uniform(keys[10], (TARGETS, LATENTS, D), jnp.float32) ** level_of(keys[10], (TARGETS, LATENTS, D), ((1, 16), (2, 2)), -0.2, 0.2)), 3.0, 300.0),
    }


def smooth(pre):
    return jax.nn.softplus(4.0 * pre) * 0.25

def adam(weight, grad, first, second):
    first_new = 0.9 * first + 0.1 * grad
    second_new = 0.999 * second + 0.001 * grad * grad
    fix_one = 1.0 - 0.9 ** STEP
    fix_two = 1.0 - 0.999 ** STEP
    weight_new = weight - 0.001 * (first_new / fix_one) / (jnp.sqrt(second_new / fix_two) + 1e-08)
    return (weight_new, first_new, second_new)

def reference(buffer_src, buffer_tgt, batch_rows, enc_w, enc_b, dec_w, dec_b, enc_m, enc_v, dec_m, dec_v):
    source = buffer_src[batch_rows]
    target = buffer_tgt[batch_rows]
    enc_half = enc_w.astype(jnp.bfloat16)
    dec_half = dec_w.astype(jnp.bfloat16)
    pre = jnp.dot(source, enc_half, preferred_element_type=jnp.float32) + enc_b
    act = smooth(pre).astype(jnp.bfloat16)
    slope = jax.nn.sigmoid(4.0 * pre)
    grads = []
    grad_act = jnp.zeros(pre.shape, jnp.float32)
    for layer in range(TARGETS):
        pred = jnp.dot(act, dec_half[layer], preferred_element_type=jnp.float32) + dec_b[layer]
        err = (pred - target[:, layer].astype(jnp.float32)).astype(jnp.bfloat16)
        grads.append(jnp.dot(act.T, err, preferred_element_type=jnp.float32))
        grad_act = grad_act + jnp.dot(err, dec_half[layer].T, preferred_element_type=jnp.float32)
    grad_dec = jnp.stack(grads, 0)
    grad_pre = (grad_act * slope).astype(jnp.bfloat16)
    grad_enc = jnp.dot(source.T, grad_pre, preferred_element_type=jnp.float32)
    enc_w_new, enc_m_new, enc_v_new = adam(enc_w, grad_enc, enc_m, enc_v)
    dec_w_new, dec_m_new, dec_v_new = adam(dec_w, grad_dec, dec_m, dec_v)
    return (enc_w_new, enc_m_new, enc_v_new, dec_w_new, dec_m_new, dec_v_new)
```

```python
import functools

import jax
import jax.numpy as jnp
from jax import lax
from jax.experimental import pallas as pl
from jax.experimental.pallas import tpu as pltpu
from jax.sharding import PartitionSpec as P

STEP = 100
FIX_ONE = 1.0 - 0.9**STEP
FIX_TWO = 1.0 - 0.999**STEP
VMEM_LIMIT = 48 * 1024 * 1024


def adam_into(grad, w_ref, m_ref, v_ref, w_out, m_out, v_out):
    first_new = 0.9 * m_ref[...] + 0.1 * grad
    second_new = 0.999 * v_ref[...] + 0.001 * grad * grad
    m_out[...] = first_new
    v_out[...] = second_new
    w_out[...] = w_ref[...] - 0.001 * (first_new * (1.0 / FIX_ONE)) / (
        jnp.sqrt(second_new * (1.0 / FIX_TWO)) + 1e-08
    )


def over_tokens(a, b):
    return lax.dot_general(a, b, (((0,), (0,)), ((), ())), preferred_element_type=jnp.float32)


def dec_kernel(act_a, act_b, err_a, err_b, w_ref, m_ref, v_ref, *rest):
    w_out, m_out, v_out = rest[-3:]
    grad = jnp.dot(act_a[...], err_a[...], preferred_element_type=jnp.float32)
    grad = grad + jnp.dot(act_b[...], err_b[...], preferred_element_type=jnp.float32)
    adam_into(grad, w_ref, m_ref, v_ref, w_out, m_out, v_out)


def dec_update(layer, act_ts, errs, dec_w, dec_m, dec_v, before):
    layers, lats, width = dec_w.shape
    block = 256 if width % 256 == 0 else 128
    whole = [pl.BlockSpec(a.shape, lambda j: (0, 0)) for a in act_ts]
    cols = [pl.BlockSpec((e.shape[0], block), lambda j: (0, j)) for e in errs]
    tile = pl.BlockSpec((None, lats, block), lambda j: (layer, 0, j))
    held = [pl.BlockSpec(memory_space=pl.ANY)] * len(before)
    tokens = sum(e.shape[0] for e in errs)
    return pl.pallas_call(
        dec_kernel,
        grid=(width // block,),
        in_specs=whole + cols + [tile] * 3 + held,
        out_specs=[tile] * 3,
        out_shape=[jax.ShapeDtypeStruct(dec_w.shape, jnp.float32)] * 3,
        input_output_aliases={7 + i: i for i in range(len(before))},
        compiler_params=pltpu.CompilerParams(vmem_limit_bytes=VMEM_LIMIT),
        cost_estimate=pl.CostEstimate(
            flops=2 * tokens * lats * width,
            bytes_accessed=24 * lats * width + 2 * tokens * width,
            transcendentals=lats * width,
        ),
        name="dec_update",
    )(*act_ts, *errs, dec_w, dec_m, dec_v, *before)


def enc_kernel(src_a, src_b, gp_a, gp_b, w_ref, m_ref, v_ref, w_out, m_out, v_out):
    grad = over_tokens(src_a[...], gp_a[...]) + over_tokens(src_b[...], gp_b[...])
    adam_into(grad, w_ref, m_ref, v_ref, w_out, m_out, v_out)


def enc_update(srcs, gps, enc_w, enc_m, enc_v):
    width, lats = enc_w.shape
    block = 256 if width % 256 == 0 else 128
    whole = [pl.BlockSpec(g.shape, lambda j: (0, 0)) for g in gps]
    cols = [pl.BlockSpec((s.shape[0], block), lambda j: (0, j)) for s in srcs]
    tile = pl.BlockSpec((block, lats), lambda j: (j, 0))
    return pl.pallas_call(
        enc_kernel,
        grid=(width // block,),
        in_specs=cols + whole + [tile] * 3,
        out_specs=[tile] * 3,
        out_shape=[jax.ShapeDtypeStruct(enc_w.shape, jnp.float32)] * 3,
        compiler_params=pltpu.CompilerParams(vmem_limit_bytes=VMEM_LIMIT),
        name="enc_update",
    )(*srcs, *gps, enc_w, enc_m, enc_v)


def on_device(
    buffer_src, buffer_tgt, batch_rows, enc_w, enc_b, dec_w, dec_b, enc_m, enc_v, dec_m, dec_v
):
    lat_count = lax.axis_size("lat")
    wid_count = lax.axis_size("wid")
    lat_place = lax.axis_index("lat")
    core = lat_place % 2
    rows = buffer_src.shape[0]
    share = -(-rows // 16) * 16
    extra = share - rows
    layers = dec_w.shape[0]
    bf16 = jnp.bfloat16
    alike = [list(range(c, lat_count, 2)) for c in range(2)]
    partner = [(i, i ^ 1) for i in range(lat_count)]

    def swap(x):
        return lax.ppermute(x, "lat", partner)

    def across(x):
        low = x.astype(bf16)
        total = x
        for hop in range(1, wid_count):
            ring = [(i, (i + hop) % wid_count) for i in range(wid_count)]
            total = total + lax.ppermute(low, "wid", ring).astype(jnp.float32)
        return total

    def gather(x):
        mine = lax.all_gather(x, "lat", axis=0, tiled=True, axis_index_groups=alike)
        return mine, swap(mine)

    own = lat_place * rows + jnp.arange(rows, dtype=batch_rows.dtype)
    chosen = jnp.any(own[:, None] == batch_rows[None, :], axis=1)
    chosen = jnp.pad(chosen, (0, extra))[:, None]
    target = jnp.pad(buffer_tgt, ((0, extra), (0, 0), (0, 0)))

    srcs = gather(jnp.pad(buffer_src, ((0, extra), (0, 0))))
    enc_half = enc_w.astype(bf16)
    dec_half = [dec_w[k].astype(bf16) for k in range(layers)]
    acts, slopes = [], []
    for src in srcs:
        pre = across(jnp.dot(src, enc_half, preferred_element_type=jnp.float32)) + enc_b
        acts.append((jax.nn.softplus(4.0 * pre) * 0.25).astype(bf16))
        slopes.append(jax.nn.sigmoid(4.0 * pre))
    act_ts = [a.T for a in acts]

    errs = []
    for k in range(layers):
        theirs = jnp.dot(acts[1], dec_half[k], preferred_element_type=jnp.float32).astype(bf16)
        mine = jnp.dot(acts[0], dec_half[k], preferred_element_type=jnp.float32)
        both = (mine + swap(theirs).astype(jnp.float32)).astype(bf16)
        pred = lax.psum_scatter(
            both, "lat", scatter_dimension=0, tiled=True, axis_index_groups=alike
        )
        err = pred.astype(jnp.float32) + dec_b[k][None] - target[:, k].astype(jnp.float32)
        errs.append(gather(jnp.where(chosen, err, 0.0).astype(bf16)))

    dec_new = ()
    for k in range(layers):
        dec_new = dec_update(k, act_ts, errs[k], dec_w, dec_m, dec_v, dec_new)

    gps = []
    for half in range(2):
        back = sum(
            lax.dot_general(
                errs[k][half],
                dec_half[k],
                (((1,), (1,)), ((), ())),
                preferred_element_type=jnp.float32,
            )
            for k in range(layers)
        )
        gps.append((across(back) * slopes[half]).astype(bf16))
    enc_new = enc_update(srcs, gps, enc_w, enc_m, enc_v)
    return (*enc_new, *dec_new)


def solution(mesh):
    placed = (
        P("lat", "wid"),
        P("lat", None, "wid"),
        P(),
        P("wid", "lat"),
        P("lat"),
        P(None, "lat", "wid"),
        P(None, "wid"),
        P("wid", "lat"),
        P("wid", "lat"),
        P(None, "lat", "wid"),
        P(None, "lat", "wid"),
    )
    return jax.shard_map(
        on_device,
        mesh=mesh,
        in_specs=placed,
        out_specs=(
            P("wid", "lat"),
            P("wid", "lat"),
            P("wid", "lat"),
            P(None, "lat", "wid"),
            P(None, "lat", "wid"),
            P(None, "lat", "wid"),
        ),
        check_vma=False,
    )
```

```python
import functools

import jax
import jax.numpy as jnp
from jax import lax
from jax.experimental import pallas as pl
from jax.experimental.pallas import tpu as pltpu
from jax.sharding import PartitionSpec as P

STEP = 100
FIX_ONE = 1.0 - 0.9**STEP
FIX_TWO = 1.0 - 0.999**STEP
VMEM_LIMIT = 48 * 1024 * 1024


def adam_into(grad, w_ref, m_ref, v_ref, w_out, m_out, v_out):
    first_new = 0.9 * m_ref[...] + 0.1 * grad
    second_new = 0.999 * v_ref[...] + 0.001 * grad * grad
    m_out[...] = first_new
    v_out[...] = second_new
    w_out[...] = w_ref[...] - 0.001 * (first_new * (1.0 / FIX_ONE)) / (
        jnp.sqrt(second_new * (1.0 / FIX_TWO)) + 1e-08
    )


def over_tokens(a, b):
    return lax.dot_general(a, b, (((0,), (0,)), ((), ())), preferred_element_type=jnp.float32)


def dec_kernel(pieces, act_t, *refs):
    errs = jnp.concatenate([r[...] for r in refs[:pieces]], axis=0)
    w_ref, m_ref, v_ref = refs[pieces : pieces + 3]
    grad = jnp.dot(act_t[...], errs, preferred_element_type=jnp.float32)
    adam_into(grad, w_ref, m_ref, v_ref, *refs[-3:])


def dec_update(layer, act_t, errs, dec_w, dec_m, dec_v, before):
    layers, lats, width = dec_w.shape
    block = 256 if width % 256 == 0 else 64
    if block == 64:
        block = width
    whole = [pl.BlockSpec(act_t.shape, lambda j: (0, 0))]
    cols = [pl.BlockSpec((e.shape[0], block), lambda j: (0, j)) for e in errs]
    tile = pl.BlockSpec((None, lats, block), lambda j: (layer, 0, j))
    held = [pl.BlockSpec(memory_space=pl.ANY)] * len(before)
    tokens = act_t.shape[1]
    return pl.pallas_call(
        functools.partial(dec_kernel, len(errs)),
        grid=(width // block,),
        in_specs=whole + cols + [tile] * 3 + held,
        out_specs=[tile] * 3,
        out_shape=[jax.ShapeDtypeStruct(dec_w.shape, jnp.float32)] * 3,
        input_output_aliases={4 + len(errs) + i: i for i in range(len(before))},
        compiler_params=pltpu.CompilerParams(vmem_limit_bytes=VMEM_LIMIT),
        cost_estimate=pl.CostEstimate(
            flops=2 * tokens * lats * width,
            bytes_accessed=24 * lats * width + 2 * tokens * width,
            transcendentals=lats * width,
        ),
        name="dec_update",
    )(act_t, *errs, dec_w, dec_m, dec_v, *before)


def enc_kernel(pieces, *refs):
    src = jnp.concatenate([r[...] for r in refs[:pieces]], axis=0)
    gp = jnp.concatenate([r[...] for r in refs[pieces : 2 * pieces]], axis=0)
    adam_into(over_tokens(src, gp), *refs[2 * pieces :])


def enc_update(srcs, gps, enc_w, enc_m, enc_v):
    width, lats = enc_w.shape
    block = 256 if width % 256 == 0 else 64
    if block == 64:
        block = width
    whole = [pl.BlockSpec(g.shape, lambda j: (0, 0)) for g in gps]
    cols = [pl.BlockSpec((s.shape[0], block), lambda j: (0, j)) for s in srcs]
    tile = pl.BlockSpec((block, lats), lambda j: (j, 0))
    return pl.pallas_call(
        functools.partial(enc_kernel, len(srcs)),
        grid=(width // block,),
        in_specs=cols + whole + [tile] * 3,
        out_specs=[tile] * 3,
        out_shape=[jax.ShapeDtypeStruct(enc_w.shape, jnp.float32)] * 3,
        compiler_params=pltpu.CompilerParams(vmem_limit_bytes=VMEM_LIMIT),
        name="enc_update",
    )(*srcs, *gps, enc_w, enc_m, enc_v)


def on_device(
    buffer_src, buffer_tgt, batch_rows, enc_w, enc_b, dec_w, dec_b, enc_m, enc_v, dec_m, dec_v
):
    lat_count = lax.axis_size("lat")
    wid_count = lax.axis_size("wid")
    lat_place = lax.axis_index("lat")
    steps = lat_count // 4
    rows = buffer_src.shape[0]
    share = -(-rows // 16) * 16
    extra = share - rows
    layers = dec_w.shape[0]
    bf16 = jnp.bfloat16
    f32 = jnp.float32

    def swap(x):
        return lax.ppermute(x, "lat", [(i, i ^ 1) for i in range(lat_count)])

    def cross(x):
        return lax.ppermute(x, "lat", [(i, i ^ 2) for i in range(lat_count)])

    def shift(x, by):
        return lax.ppermute(x, "lat", [(i, (i + 4 * by) % lat_count) for i in range(lat_count)])

    def across(x):
        low = x.astype(bf16)
        total = x
        for hop in range(1, wid_count):
            ring = [(i, (i + hop) % wid_count) for i in range(wid_count)]
            total = total + lax.ppermute(low, "wid", ring).astype(f32)
        return total

    def along(x):
        return jnp.concatenate([x] + [shift(x, s) for s in range(1, steps)], axis=0)

    def dot(a, b):
        return jnp.dot(a, b, preferred_element_type=f32)

    own = lat_place * rows + jnp.arange(rows, dtype=batch_rows.dtype)
    chosen = jnp.any(own[:, None] == batch_rows[None, :], axis=1)
    chosen = jnp.pad(chosen, (0, extra))[:, None]
    target = jnp.pad(buffer_tgt, ((0, extra), (0, 0), (0, 0)))

    near = along(jnp.pad(buffer_src, ((0, extra), (0, 0))))
    far = cross(near)
    srcs = [near, swap(near), far, swap(far)]
    enc_half = enc_w.astype(bf16)
    dec_half = [dec_w[k].astype(bf16) for k in range(layers)]
    acts, slopes = [], []
    for src in srcs:
        pre = across(dot(src, enc_half)) + enc_b
        acts.append((jax.nn.softplus(4.0 * pre) * 0.25).astype(bf16))
        slopes.append(jax.nn.sigmoid(4.0 * pre))
    act_t = jnp.concatenate(acts, axis=0).T

    nears, fars = [], []
    for k in range(layers):
        both = []
        for side in (1, 0):
            theirs = swap(dot(acts[2 * side + 1], dec_half[k]).astype(bf16))
            both.append(dot(acts[2 * side], dec_half[k]) + theirs.astype(f32))
        total = both[1] + cross(both[0].astype(bf16)).astype(f32)
        low = total.astype(bf16)
        pred = total[:share]
        for s in range(1, steps):
            pred = pred + shift(low[s * share : (s + 1) * share], -s).astype(f32)
        goal, keep, bias = lax.optimization_barrier((target[:, k], chosen, dec_b[k]))
        err = pred + bias[None] - goal.astype(f32)
        near = along(jnp.where(keep, err, 0.0).astype(bf16))
        nears.append(near)
        fars.append(cross(near))

    errs = []
    backs = [0.0] * 4
    dec_new = ()
    for k in range(layers):
        near, far = nears[k], fars[k]
        errs.append([near, swap(near), far, swap(far)])
        for i in range(4):
            backs[i] = backs[i] + lax.dot_general(
                errs[k][i], dec_half[k], (((1,), (1,)), ((), ())), preferred_element_type=f32
            )
        dec_new = dec_update(k, act_t, errs[k], dec_w, dec_m, dec_v, dec_new)

    gps = [(across(backs[i]) * slopes[i]).astype(bf16) for i in range(4)]
    enc_new = enc_update(srcs, gps, enc_w, enc_m, enc_v)
    return (*enc_new, *dec_new)


def solution(mesh):
    placed = (
        P("lat", "wid"),
        P("lat", None, "wid"),
        P(),
        P("wid", "lat"),
        P("lat"),
        P(None, "lat", "wid"),
        P(None, "wid"),
        P("wid", "lat"),
        P("wid", "lat"),
        P(None, "lat", "wid"),
        P(None, "lat", "wid"),
    )
    return jax.shard_map(
        on_device,
        mesh=mesh,
        in_specs=placed,
        out_specs=(
            P("wid", "lat"),
            P("wid", "lat"),
            P("wid", "lat"),
            P(None, "lat", "wid"),
            P(None, "lat", "wid"),
            P(None, "lat", "wid"),
        ),
        check_vma=False,
    )
```

```python
import functools

import jax
import jax.numpy as jnp
from jax import lax
from jax.experimental import pallas as pl
from jax.experimental.pallas import tpu as pltpu
from jax.sharding import PartitionSpec as P

STEP = 100
FIX_ONE = 1.0 - 0.9**STEP
FIX_TWO = 1.0 - 0.999**STEP
VMEM_LIMIT = 48 * 1024 * 1024


def adam_into(grad, w_ref, m_ref, v_ref, w_out, m_out, v_out):
    first_new = 0.9 * m_ref[...] + 0.1 * grad
    second_new = 0.999 * v_ref[...] + 0.001 * grad * grad
    m_out[...] = first_new
    v_out[...] = second_new
    w_out[...] = w_ref[...] - 0.001 * (first_new * (1.0 / FIX_ONE)) / (
        jnp.sqrt(second_new * (1.0 / FIX_TWO)) + 1e-08
    )


def over_tokens(a, b):
    return lax.dot_general(a, b, (((0,), (0,)), ((), ())), preferred_element_type=jnp.float32)


def dec_kernel(pieces, act_t, *refs):
    errs = jnp.concatenate([r[...] for r in refs[:pieces]], axis=0)
    w_ref, m_ref, v_ref = refs[pieces : pieces + 3]
    grad = jnp.dot(act_t[...], errs, preferred_element_type=jnp.float32)
    adam_into(grad, w_ref, m_ref, v_ref, *refs[-3:])


def dec_update(layer, act_t, errs, dec_w, dec_m, dec_v, before):
    layers, lats, width = dec_w.shape
    block = 256 if width % 256 == 0 else 64
    if block == 64:
        block = width
    whole = [pl.BlockSpec(act_t.shape, lambda j: (0, 0))]
    cols = [pl.BlockSpec((e.shape[0], block), lambda j: (0, j)) for e in errs]
    tile = pl.BlockSpec((None, lats, block), lambda j: (layer, 0, j))
    held = [pl.BlockSpec(memory_space=pl.ANY)] * len(before)
    tokens = act_t.shape[1]
    return pl.pallas_call(
        functools.partial(dec_kernel, len(errs)),
        grid=(width // block,),
        in_specs=whole + cols + [tile] * 3 + held,
        out_specs=[tile] * 3,
        out_shape=[jax.ShapeDtypeStruct(dec_w.shape, jnp.float32)] * 3,
        input_output_aliases={4 + len(errs) + i: i for i in range(len(before))},
        compiler_params=pltpu.CompilerParams(vmem_limit_bytes=VMEM_LIMIT),
        cost_estimate=pl.CostEstimate(
            flops=2 * tokens * lats * width,
            bytes_accessed=24 * lats * width + 2 * tokens * width,
            transcendentals=lats * width,
        ),
        name="dec_update",
    )(act_t, *errs, dec_w, dec_m, dec_v, *before)


def enc_kernel(pieces, *refs):
    src = jnp.concatenate([r[...] for r in refs[:pieces]], axis=0)
    gp = jnp.concatenate([r[...] for r in refs[pieces : 2 * pieces]], axis=0)
    adam_into(over_tokens(src, gp), *refs[2 * pieces :])


def enc_update(srcs, gps, enc_w, enc_m, enc_v):
    width, lats = enc_w.shape
    block = 256 if width % 256 == 0 else 64
    if block == 64:
        block = width
    whole = [pl.BlockSpec(g.shape, lambda j: (0, 0)) for g in gps]
    cols = [pl.BlockSpec((s.shape[0], block), lambda j: (0, j)) for s in srcs]
    tile = pl.BlockSpec((block, lats), lambda j: (j, 0))
    return pl.pallas_call(
        functools.partial(enc_kernel, len(srcs)),
        grid=(width // block,),
        in_specs=cols + whole + [tile] * 3,
        out_specs=[tile] * 3,
        out_shape=[jax.ShapeDtypeStruct(enc_w.shape, jnp.float32)] * 3,
        compiler_params=pltpu.CompilerParams(vmem_limit_bytes=VMEM_LIMIT),
        name="enc_update",
    )(*srcs, *gps, enc_w, enc_m, enc_v)


def on_device(
    buffer_src, buffer_tgt, batch_rows, enc_w, enc_b, dec_w, dec_b, enc_m, enc_v, dec_m, dec_v
):
    lat_count = lax.axis_size("lat")
    wid_count = lax.axis_size("wid")
    lat_place = lax.axis_index("lat")
    steps = lat_count // 4
    rows = buffer_src.shape[0]
    share = -(-rows // 16) * 16
    extra = share - rows
    layers = dec_w.shape[0]
    bf16 = jnp.bfloat16
    f32 = jnp.float32

    def swap(x):
        return lax.ppermute(x, "lat", [(i, i ^ 1) for i in range(lat_count)])

    def cross(x):
        return lax.ppermute(x, "lat", [(i, i ^ 2) for i in range(lat_count)])

    def shift(x, by):
        return lax.ppermute(x, "lat", [(i, (i + 4 * by) % lat_count) for i in range(lat_count)])

    def across(x):
        low = x.astype(bf16)
        total = x
        for hop in range(1, wid_count):
            ring = [(i, (i + hop) % wid_count) for i in range(wid_count)]
            total = total + lax.ppermute(low, "wid", ring).astype(f32)
        return total

    def along(x):
        return jnp.concatenate([x] + [shift(x, s) for s in range(1, steps)], axis=0)

    def after(x, *first):
        return lax.optimization_barrier((x, *first))[0]

    def dot(a, b):
        return jnp.dot(a, b, preferred_element_type=f32)

    own = lat_place * rows + jnp.arange(rows, dtype=batch_rows.dtype)
    chosen = jnp.any(own[:, None] == batch_rows[None, :], axis=1)
    chosen = jnp.pad(chosen, (0, extra))[:, None]
    target = jnp.pad(buffer_tgt, ((0, extra), (0, 0), (0, 0)))

    near = along(jnp.pad(buffer_src, ((0, extra), (0, 0))))
    far = cross(near)
    enc_half = enc_w.astype(bf16)
    srcs = [near, swap(near)]
    parts = [across(dot(src, enc_half)) for src in srcs]
    far = after(far, *parts)
    srcs += [far, swap(far)]
    parts += [across(dot(src, enc_half)) for src in srcs[2:]]
    dec_half = [dec_w[k].astype(bf16) for k in range(layers)]
    acts, slopes = [], []
    for part in parts:
        pre = part + enc_b
        acts.append((jax.nn.softplus(4.0 * pre) * 0.25).astype(bf16))
        slopes.append(jax.nn.sigmoid(4.0 * pre))
    act_t = jnp.concatenate(acts, axis=0).T

    sums, came = [], []
    for k in range(layers):
        both = []
        for side in (1, 0):
            theirs = swap(dot(acts[2 * side + 1], dec_half[k]).astype(bf16))
            both.append(dot(acts[2 * side], dec_half[k]) + theirs.astype(f32))
        sums.append(both[1])
        came.append(cross(both[0].astype(bf16)))

    mine = []
    for k in range(layers):
        got = after(came[k], mine[k - 2]) if k >= 2 else came[k]
        total = sums[k] + got.astype(f32)
        low = total.astype(bf16)
        pred = total[:share]
        for s in range(1, steps):
            pred = pred + shift(low[s * share : (s + 1) * share], -s).astype(f32)
        goal, keep, bias = lax.optimization_barrier((target[:, k], chosen, dec_b[k]))
        err = pred + bias[None] - goal.astype(f32)
        mine.append(jnp.where(keep, err, 0.0).astype(bf16))

    nears, fars = [], []
    for k in range(layers):
        near = along(after(mine[k], nears[k - 1]) if k else mine[k])
        nears.append(near)
        fars.append(cross(near))

    errs = []
    backs = [0.0] * 4
    dec_new = ()
    for k in range(layers):
        near, far = nears[k], fars[k]
        if k == layers - 1 and k:
            far, *dec_new = lax.optimization_barrier((far, *dec_new))
        errs.append([near, swap(near), far, swap(far)])
        for i in range(4):
            backs[i] = backs[i] + lax.dot_general(
                errs[k][i], dec_half[k], (((1,), (1,)), ((), ())), preferred_element_type=f32
            )
        dec_new = dec_update(k, act_t, errs[k], dec_w, dec_m, dec_v, dec_new)

    gps = [(across(backs[i]) * slopes[i]).astype(bf16) for i in range(4)]
    enc_new = enc_update(srcs, gps, enc_w, enc_m, enc_v)
    return (*enc_new, *dec_new)


def solution(mesh):
    placed = (
        P("lat", "wid"),
        P("lat", None, "wid"),
        P(),
        P("wid", "lat"),
        P("lat"),
        P(None, "lat", "wid"),
        P(None, "wid"),
        P("wid", "lat"),
        P("wid", "lat"),
        P(None, "lat", "wid"),
        P(None, "lat", "wid"),
    )
    return jax.shard_map(
        on_device,
        mesh=mesh,
        in_specs=placed,
        out_specs=(
            P("wid", "lat"),
            P("wid", "lat"),
            P("wid", "lat"),
            P(None, "lat", "wid"),
            P(None, "lat", "wid"),
            P(None, "lat", "wid"),
        ),
        check_vma=False,
    )
```
